32 devices in a mesh: seq: 16 (over z, y, x), head: 2 (over core).
Axes of the slice: x: 2, y: 2, z: 4, core: 2. Of those that a mesh axis runs over, the one named last changes fastest.
Arguments:
- token_values: bfloat16 [8192, 3072], P('seq', 'head'), may hold values from -6 to 6
- step_logits: bfloat16 [8192, 48], P('seq', 'head'), may hold values from -4 to 8
- write_keys: bfloat16 [8192, 128], P('seq'), may hold values from -6 to 6
- read_queries: bfloat16 [8192, 128], P('seq'), may hold values from -1.5 to 1.5
- target: int32 [8192], P('seq'), may hold values from 0 to 8191, as said below
- doc_lengths: int32 [8], replicated, may hold values from 1 to 4096, 8192 in all
- decay_log: float32 [48], P('head'), may hold values from -12 to 1.4
- step_bias: float32 [48], P('head'), may hold values from -5.5 to -3.5
- skip_gain: float32 [48], P('head'), may hold values from 0.1 to 1.9
- init_state: float32 [48, 64, 128], P('head'), may hold values from -6 to 6
- out_grad: bfloat16 [8192, 3072], P('seq', 'head'), may hold values from -0.59765625 to 0.59765625
Outputs:
- layer_out: bfloat16 [8192, 3072], P('seq', 'head')
- grad_values: bfloat16 [8192, 3072], P('seq', 'head')
- grad_logits: float32 [8192, 48], P('seq', 'head')
- grad_write: float32 [8192, 128], P('seq')
- grad_read: float32 [8192, 128], P('seq')
The draws below stay inside these ranges and needn't reach their ends.
Inputs may be any that keep to these rules, and one draw needn't show every extreme that they name: target holds every sequence position once. Group the rows by the index of seq that holds them and by target // 512: each group has at most 64 rows, every index of seq sends the same multiset of group sizes and receives the same multiset, and the largest group has exactly 64 rows. `doc_lengths`: the lengths sum to 8192; the longest is exactly 4096.
All inputs are finite; a program needn't handle non-finite values.
Results may differ from the reference program's by a relative error of at most 0.001.
Values may be sent and summed in bfloat16 or wider, within the bound.
No kernel may reach another device: no remote copies, remote signals or barrier semaphores. Data moves between devices by JAX's collectives and lax.ppermute only.
A program may use at most 128 MiB of HBM per device.

```python
import math
from functools import partial
import jax
import jax.numpy as jnp
import numpy as np
from jax import lax

HEADS = 48
HEAD_DIM = 64
STATE_DIM = 128
TOK_DEV = 512
BLOCK = 256
DOCS = 8
WINDOW_TOKENS = 8192


def draw_target(key, part):
    dev_count = WINDOW_TOKENS // TOK_DEV
    mean_rows = TOK_DEV // dev_count
    key_a, second_random_key, key_c, key_d, key_e = jax.random.split(jax.random.fold_in(key, 11), 5)
    offsets = jax.random.randint(key_a, (dev_count // 2,), 0, mean_rows + 1)
    offsets = offsets.at[0].set(mean_rows)
    sizes_list = jnp.stack([mean_rows + offsets, mean_rows - offsets], axis=1).reshape(dev_count)
    relabel = jax.random.permutation(second_random_key, dev_count)
    row_perm = jax.random.permutation(key_c, dev_count)
    col_perm = jax.random.permutation(key_d, dev_count)
    counts = sizes_list[relabel[jnp.bitwise_xor(row_perm[:, None], col_perm[None, :])]]
    arrive_before = jnp.cumsum(counts, axis=0) - counts
    send_end = jnp.cumsum(counts, axis=1)
    send_start = send_end - counts
    row_ids = jnp.arange(TOK_DEV, dtype=jnp.int32)
    dest_dev = jnp.sum((send_end[:, None, :] <= row_ids[None, :, None]).astype(jnp.int32), axis=2)
    begin_row = jnp.take_along_axis(send_start, dest_dev, axis=1)
    offset_in = jnp.take_along_axis(arrive_before, dest_dev, axis=1)
    ordered = dest_dev * TOK_DEV + offset_in + (row_ids[None, :] - begin_row)
    shuffle_keys = jax.random.split(key_e, dev_count)
    shuffles = jax.vmap(lambda child_random_key: jax.random.permutation(child_random_key, TOK_DEV))(shuffle_keys)
    return jnp.take_along_axis(ordered, shuffles, axis=1).reshape(WINDOW_TOKENS).astype(jnp.int32)


def draw_decay_log(key, part):
    key_a, second_random_key, key_c = jax.random.split(jax.random.fold_in(key, 23), 3)
    slow_share = 0.5
    slow_head = jax.random.uniform(key_a, (HEADS,), jnp.float32) < slow_share
    slow_rate = jnp.exp(jax.random.uniform(second_random_key, (HEADS,), jnp.float32, math.log(3.0), math.log(30.0))) / WINDOW_TOKENS
    fast_rate = jnp.exp(jax.random.uniform(key_c, (HEADS,), jnp.float32, 0.0, math.log(4.0)))
    return jnp.log(jnp.where(slow_head, slow_rate, fast_rate)).astype(jnp.float32)


def draw_step_logits(key, part):
    key_a, second_random_key = jax.random.split(jax.random.fold_in(key, 37), 2)
    baseline_portion = jnp.clip(jax.random.normal(key_a, (WINDOW_TOKENS, HEADS), jnp.float32), -4.0, 4.0)
    spike_portion = (jax.random.uniform(second_random_key, (WINDOW_TOKENS, 1), jnp.float32) < 1.0 / 4096.0).astype(jnp.float32) * 4.0
    return (baseline_portion + spike_portion).astype(jnp.bfloat16)


def steps_of(own_key, dims, cuts, low, high):
    loudness, own = 1.0, jax.random.fold_in(own_key, 6)
    for axis_at, parts in cuts:
        heights = jnp.exp(jax.random.uniform(jax.random.fold_in(own, axis_at), (parts,), jnp.float32, low / len(cuts), high / len(cuts)))
        loudness = loudness * jnp.repeat(heights, dims[axis_at] // parts).reshape([-1 if axis == axis_at else 1 for axis in range(len(dims))])
    return loudness


def length_profile(amount, total, bound, skew):
    portions = [(1 << 20) // math.isqrt(grade ** skew) + 1 for grade in range(2, amount + 1)]
    surplus, holding = total - bound - (amount - 1), [1] * (amount - 1)
    while surplus > 0:
        candidates = [i for i in range(amount - 1) if holding[i] < bound]
        whole, remaining = sum([portions[i] for i in candidates]), surplus
        for i in candidates:
            extra = min(bound - holding[i], max(1, remaining * portions[i] // whole), surplus)
            holding[i] = holding[i] + extra
            surplus = surplus - extra
    return np.array([bound] + holding)


def uneven(stream_key, count, total, reach, slope):
    if count == 2:
        one = jax.random.randint(stream_key, (), max(1, total - reach), min(reach, total - 1) + 1)
        return jnp.stack([one, total - one])
    tallies = jnp.asarray(length_profile(count, total, reach, slope), jnp.int32)
    pairs = (count - 1) // 2
    donor, sink = tallies[1:1 + 2 * pairs:2], tallies[2:2 + 2 * pairs:2]
    margin = jnp.minimum(donor - 1, reach - sink)
    shifted = jax.random.randint(jax.random.fold_in(stream_key, 1), (pairs,), 0, 1 << 20) % (margin + 1)
    tallies = tallies.at[1:1 + 2 * pairs:2].set(donor - shifted).at[2:2 + 2 * pairs:2].set(sink + shifted)
    return tallies[jax.random.permutation(jax.random.fold_in(stream_key, 2), count)]


def normal_values(stream_key, shape, width, bound, shards=(), kind=jnp.bfloat16):
    result = width * jax.random.normal(stream_key, shape, jnp.float32)
    if shards:
        result = result * steps_of(stream_key, shape, shards, -0.22, 0.18)
    return jnp.clip(result, -bound, bound).astype(kind)


def setup_inputs(seed: int = 0) -> dict:
    splits = jax.random.split(jax.random.key(seed), 12)
    token_values = normal_values(splits[0], (WINDOW_TOKENS, HEADS * HEAD_DIM), 1.0, 6.0, ((0, 16), (1, 2)))
    step_logits = draw_step_logits(jax.random.fold_in(splits[11], 71), 0)
    write_keys = normal_values(splits[2], (WINDOW_TOKENS, STATE_DIM), 1.0, 6.0, ((0, 16),))
    read_queries = normal_values(splits[3], (WINDOW_TOKENS, STATE_DIM), 0.25, 1.5, ((0, 16),))
    target = draw_target(jax.random.fold_in(splits[11], 71), 0)
    doc_lengths = uneven(splits[5], DOCS, WINDOW_TOKENS, WINDOW_TOKENS // 2, 2).astype(jnp.int32)
    decay_log = draw_decay_log(jax.random.fold_in(splits[11], 71), 0)
    step_bias = jnp.clip(-5.5 + 2.0 * jax.random.uniform(splits[7], (HEADS,), jnp.float32) ** steps_of(splits[7], (HEADS,), ((0, 2),), -0.2, 0.2), -5.5, -3.5)
    skip_gain = jnp.clip(1.0 + 0.18 * jax.random.normal(splits[8], (HEADS,), jnp.float32), 0.1, 1.9)
    init_state = normal_values(splits[9], (HEADS, HEAD_DIM, STATE_DIM), 1.0, 6.0, ((0, 2),), jnp.float32)
    out_grad = normal_values(splits[10], (WINDOW_TOKENS, HEADS * HEAD_DIM), 0.1, 0.59765625, ((0, 16), (1, 2)))
    return {"token_values": token_values, "step_logits": step_logits, "write_keys": write_keys, "read_queries": read_queries, "target": target, "doc_lengths": doc_lengths, "decay_log": decay_log, "step_bias": step_bias, "skip_gain": skip_gain, "init_state": init_state, "out_grad": out_grad}


highest = lax.Precision.HIGHEST

def block_step(carry_state, pieces, decay_rate):
    values_f, step_size, write_f, read_f, reset_int = pieces
    cum_decay = jnp.cumsum(step_size * decay_rate[None, :], axis=0)
    reset_count = jnp.cumsum(reset_int).astype(jnp.int32)
    order_pos = jnp.arange(reset_int.shape[0], dtype=jnp.int32)
    causal = (order_pos[:, None] >= order_pos[None, :]) & (reset_count[:, None] == reset_count[None, :])
    spread = cum_decay.T[:, :, None] - cum_decay.T[:, None, :]
    within = jnp.exp(jnp.where(causal[None], spread, -jnp.inf))
    scores = jnp.dot(read_f, write_f.T, precision=highest, preferred_element_type=jnp.float32)
    blend_matrix = scores[None] * within * step_size.T[:, None, :]
    inner_part = jnp.einsum('hts,shp->thp', blend_matrix, values_f, precision=highest)
    carry_in = jnp.exp(cum_decay) * (reset_count == 0).astype(jnp.float32)[:, None]
    outer_part = jnp.einsum('tn,hpn->thp', read_f, carry_state, precision=highest) * carry_in[:, :, None]
    last_decay = cum_decay[-1]
    weight = jnp.exp(last_decay[None, :] - cum_decay) * (reset_count == reset_count[-1]).astype(jnp.float32)[:, None] * step_size
    fresh_state = jnp.einsum('sh,shp,sn->hpn', weight, values_f, write_f, precision=highest)
    keep_share = jnp.exp(last_decay) * (reset_count[-1] == 0).astype(jnp.float32)
    new_state = keep_share[:, None, None] * carry_state + fresh_state
    return (new_state, inner_part + outer_part)

def ssd_layer(values_f, logits_f, write_f, read_f, reset_int, decay_log, step_bias, skip_gain, init_state):
    step_size = jax.nn.softplus(logits_f + step_bias[None, :])
    decay_rate = -jnp.exp(decay_log)
    block_count = values_f.shape[0] // BLOCK
    pieces = (values_f.reshape(block_count, BLOCK, HEADS, HEAD_DIM), step_size.reshape(block_count, BLOCK, HEADS), write_f.reshape(block_count, BLOCK, STATE_DIM), read_f.reshape(block_count, BLOCK, STATE_DIM), reset_int.reshape(block_count, BLOCK))
    step_fn = jax.checkpoint(partial(block_step, decay_rate=decay_rate))
    last_state, block_outs = lax.scan(step_fn, init_state, pieces)
    return block_outs.reshape(values_f.shape) + skip_gain[None, :, None] * values_f

def reference(token_values, step_logits, write_keys, read_queries, target, doc_lengths, decay_log, step_bias, skip_gain, init_state, out_grad):
    placed_values = jnp.zeros_like(token_values).at[target].set(token_values)
    placed_logits = jnp.zeros_like(step_logits).at[target].set(step_logits)
    placed_write = jnp.zeros_like(write_keys).at[target].set(write_keys)
    placed_read = jnp.zeros_like(read_queries).at[target].set(read_queries)
    starts = jnp.cumsum(doc_lengths).astype(jnp.int32)[:-1]
    reset_int = jnp.zeros((WINDOW_TOKENS,), jnp.int32).at[starts].set(1)
    values_f = placed_values.astype(jnp.float32).reshape(WINDOW_TOKENS, HEADS, HEAD_DIM)
    logits_f = placed_logits.astype(jnp.float32)
    write_f = placed_write.astype(jnp.float32)
    read_f = placed_read.astype(jnp.float32)

    def forward(values_in, logits_in, write_in, read_in):
        return ssd_layer(values_in, logits_in, write_in, read_in, reset_int, decay_log, step_bias, skip_gain, init_state)
    full_out, pullback = jax.vjp(forward, values_f, logits_f, write_f, read_f)
    grads = pullback(out_grad.astype(jnp.float32).reshape(WINDOW_TOKENS, HEADS, HEAD_DIM))
    layer_out = full_out.reshape(WINDOW_TOKENS, HEADS * HEAD_DIM).astype(jnp.bfloat16)
    grad_values = grads[0].reshape(WINDOW_TOKENS, HEADS * HEAD_DIM).astype(jnp.bfloat16)
    return (layer_out, grad_values, grads[1], grads[2], grads[3])
```

```python
from functools import partial

import jax
import jax.numpy as jnp
from jax import lax
from jax.experimental import pallas as pl
from jax.experimental.pallas import tpu as pltpu
from jax.sharding import PartitionSpec as P

f32 = jnp.float32
bf16 = jnp.bfloat16
LANES = 128
NEG = -1e30
LOG2E = 1.4426950408889634
GROUPS = 1


def split2(x):
    hi = x.astype(bf16)
    return hi, (x - hi.astype(f32)).astype(bf16)


def split3(x):
    hi = x.astype(bf16)
    rest = x - hi.astype(f32)
    mid = rest.astype(bf16)
    return hi, mid, (rest - mid.astype(f32)).astype(bf16)


def mm(a, b):
    return lax.dot_general(a, b, (((1,), (0,)), ((), ())), preferred_element_type=f32)


def mm_nt(a, b):
    return lax.dot_general(a, b, (((1,), (1,)), ((), ())), preferred_element_type=f32)


def iota(shape, dim):
    return lax.broadcasted_iota(jnp.int32, shape, dim)


def params(grid_dims=1):
    return pltpu.CompilerParams(
        dimension_semantics=("arbitrary",) * grid_dims, vmem_limit_bytes=56 * 1024 * 1024
    )


def whole(shape):
    return pl.BlockSpec(shape, lambda *_: (0,) * len(shape))


def dispatch_kernel(shift, capacity, trow_ref, tcol_ref, kaux_ref, oh_ref, ks_ref):
    rows = trow_ref.shape[1]
    slots = oh_ref.shape[0]
    owner_row = lax.shift_right_logical(trow_ref[...], shift)
    owner_col = lax.shift_right_logical(tcol_ref[...], shift)
    earlier = (owner_col == owner_row) & (iota((rows, rows), 0) < iota((rows, rows), 1))
    rank = jnp.sum(jnp.where(earlier, 1.0, 0.0), axis=0, keepdims=True)
    slot = owner_row * capacity + rank.astype(jnp.int32)
    onehot = jnp.where(iota((slots, rows), 0) == slot, 1.0, 0.0).astype(bf16)
    oh_ref[...] = onehot
    ks_ref[...] = mm(onehot, kaux_ref[...]).astype(bf16)


def doc_at(docs_ref, pos):
    start = jnp.int32(0)
    total = pos * 0
    for d in range(docs_ref.shape[0] - 1):
        start = start + docs_ref[d]
        total = total + jnp.where(pos >= start, 1, 0)
    return total


def row_of(ref, c, h):
    return jnp.broadcast_to(ref[c, pl.ds(h, 1), :], (LANES, LANES))


def expand_pair(ref, c, h0):
    upper = iota((LANES, LANES), 0) < LANES // 2
    return jnp.where(upper, row_of(ref, c, h0), row_of(ref, c, h0 + 1)).T


def expand_all(ref, h0):
    return jnp.concatenate([expand_pair(ref, c, h0) for c in range(ref.shape[0])], axis=0)


def setup_kernel(
    heads, lo_count, idx_ref, docs_ref, got_ref, og_ref, bias_ref, dlog_ref,
    pm_ref, b_ref, c_ref, bt_ref, ct_ref, dt_ref, sig_ref, at_ref, btt_ref, eat_ref, wt_ref,
    wdt_ref, mb_ref, keep_ref, u_ref, eadt_ref,
):
    rows = og_ref.shape[0]
    slots = got_ref.shape[0]
    n = b_ref.shape[1]
    chunks = rows // LANES
    j = pl.program_id(0)

    @pl.when(j == 0)
    def _():
        p0 = idx_ref[0] * rows
        aux_t = got_ref[:, 2 * n : 2 * n + LANES].astype(f32).T
        pos = aux_t[LANES - 3 : LANES - 2] * 16.0 + aux_t[LANES - 2 : LANES - 1]
        pos = jnp.where(aux_t[LANES - 1 : LANES] > 0.5, pos, -1.0).astype(jnp.int32)
        pm = jnp.where(iota((rows, slots), 0) == pos, 1.0, 0.0).astype(bf16)
        pm_ref[...] = pm
        placed = mm(pm, got_ref[...])
        b_all = placed[:, :n]
        c_all = placed[:, n : 2 * n]
        b_ref[...] = b_all.astype(bf16)
        c_ref[...] = c_all.astype(bf16)
        logits = placed[:, 2 * n : 2 * n + LANES]
        logits = jnp.where(iota(logits.shape, 1) < heads, logits, 0.0)
        x = logits + bias_ref[...]
        u = jnp.exp(-jnp.abs(x))
        small = u * (1.0 - u * (0.5 - u * (1.0 / 3.0 - u * (0.25 - u * 0.2))))
        dt = jnp.maximum(x, 0.0) + jnp.where(u < 0.03, small, jnp.log(1.0 + u))
        dt_ref[...] = dt
        sig_ref[...] = jnp.where(x >= 0.0, 1.0, u) / (1.0 + u)
        logdt = jnp.log(dt) * LOG2E
        z = dt * (-jnp.exp(dlog_ref[...]) * LOG2E)
        tri = jnp.where(iota((LANES, LANES), 0) >= iota((LANES, LANES), 1), 1.0, 0.0).astype(bf16)
        offs = []
        off = jnp.zeros((1, LANES), f32)
        local = []
        for c in range(chunks):
            z0, z1, z2 = split3(z[c * LANES : (c + 1) * LANES])
            a = (mm(tri, z2) + mm(tri, z1)) + mm(tri, z0)
            local.append(a)
            offs.append(off)
            off = off + a[LANES - 1 : LANES]
        doc_before = doc_at(docs_ref, p0 - 1)
        doc_last = doc_at(docs_ref, p0 + rows - 1)
        for c in range(chunks):
            at = slice(c * LANES, (c + 1) * LANES)
            q0 = p0 + c * LANES
            a = local[c]
            ld = logdt[at]
            end = a[LANES - 1 : LANES]
            doc_n = doc_at(docs_ref, q0 + iota((LANES, LANES), 0))
            doc_t = doc_at(docs_ref, q0 + iota((LANES, LANES), 1))
            causal = (doc_n == doc_t) & (iota((LANES, LANES), 0) >= iota((LANES, LANES), 1))
            mb_ref[at] = jnp.where(causal, 0.0, NEG)
            at_ref[c] = a.T
            btt_ref[c] = (a - ld).T
            eat_ref[c] = jnp.where(doc_n == doc_at(docs_ref, q0 - 1), a, NEG).T
            wt_ref[c] = jnp.where(
                doc_n == doc_at(docs_ref, q0 + LANES - 1), end - a + ld, NEG
            ).T
            full = a + offs[c]
            eadt_ref[c] = jnp.where(doc_n == doc_before, full, NEG).T
            wdt_ref[c] = jnp.where(doc_n == doc_last, off - full + ld, NEG).T
            bt_ref[:, at] = b_all[at].T.astype(bf16)
            ct_ref[:, at] = c_all[at].T.astype(bf16)

    ea = jnp.exp2(expand_all(eadt_ref, 2 * j))
    hi, lo = split2(ea * og_ref[...].astype(f32))
    ut = mm(ct_ref[...], hi) + mm(ct_ref[...], lo)
    keep = jnp.broadcast_to(ea[rows - 1 : rows], (8, LANES))
    keep_ref[...] = keep
    q = n // lo_count
    for k in range(lo_count):
        u_ref[k, :q, :] = ut[k * q : (k + 1) * q]
        u_ref[k, q:, :] = keep


def place_kernel(base, lo_count, got_ref, pm_ref, wdt_ref, bt_ref, keep_ref, v_ref, f_ref):
    rows = pm_ref.shape[0]
    v = mm(pm_ref[...], got_ref[...])
    v_ref[...] = v.astype(bf16)
    w = jnp.exp2(expand_all(wdt_ref, 2 * (base + pl.program_id(0))))
    hi, lo = split2(w * v)
    ft = mm(bt_ref[...], hi) + mm(bt_ref[...], lo)
    q = ft.shape[0] // lo_count
    for k in range(lo_count):
        f_ref[k, :q, :] = ft[k * q : (k + 1) * q]
        f_ref[k, q:, :] = keep_ref[...]


def layer_kernel(
    base, v_ref, g_ref, st_ref, ut_ref, at_ref, btt_ref, eat_ref, wt_ref, b_ref, c_ref,
    bt_ref, ct_ref, mb_ref, skip_ref,
    lout_ref, gval_ref, z_ref, dc_ref, db_ref, gy_ref, vdv_ref, end_ref,
    cb_ref, dvi_ref, ea_ref, w_ref,
):
    rows = v_ref.shape[0]
    chunks = rows // LANES
    half = LANES // 2
    j = pl.program_id(0)
    pair = base + j
    h0 = 2 * pair

    @pl.when(j == 0)
    def _():
        for c in range(chunks):
            at = slice(c * LANES, (c + 1) * LANES)
            cb_ref[at] = mm_nt(c_ref[at], b_ref[at])
        for ref in (z_ref, dc_ref, db_ref, gy_ref, vdv_ref, end_ref):
            ref[...] = jnp.zeros_like(ref)

    lane = iota((LANES, LANES), 1)
    sub = iota((LANES, LANES), 0)
    low = lane < half
    pick = jnp.where(h0 + jnp.where(sub < half, 0, 1) == lane, 1.0, 0.0).astype(bf16)
    skip = skip_ref[0:1]
    st = st_ref[...]
    for c in range(chunks):
        at = slice(c * LANES, (c + 1) * LANES)
        v = v_ref[at]
        g = g_ref[at]
        vf = v.astype(f32)
        gf = g.astype(f32)
        zero = jnp.zeros_like(v)
        gt = gf.T.astype(bf16)
        ea = jnp.exp2(expand_pair(eat_ref, c, h0))
        w = jnp.exp2(expand_pair(wt_ref, c, h0))
        ea_ref[at] = ea
        w_ref[at] = w
        cb = cb_ref[at]
        mb = mb_ref[at]
        zacc = z_ref[at]
        his, los, dvs = [], [], []
        for k in range(2):
            acol = row_of(at_ref, c, h0 + k).T
            spread = jnp.exp2(acol - row_of(btt_ref, c, h0 + k) + mb)
            mine = low if k == 0 else jnp.logical_not(low)
            gv = mm_nt(jnp.where(mine, g, zero), v)
            zacc = zacc + gv * spread
            hi, lo = split2(cb * spread)
            his.append(hi)
            los.append(lo)
            gk = gt[k * half : (k + 1) * half]
            dvs.append(mm(gk, hi) + mm(gk, lo))
        z_ref[at] = zacc
        dvi_ref[at] = jnp.concatenate(dvs, axis=0).T
        both = jnp.concatenate([jnp.where(low, v, zero), jnp.where(low, zero, v)], axis=0)
        y = mm(jnp.concatenate(his, axis=1), both) + mm(jnp.concatenate(los, axis=1), both)
        st_hi, st_lo = split2(st)
        y = y + ea * (mm(c_ref[at], st_hi) + mm(c_ref[at], st_lo))
        lout_ref[at] = (y + skip * vf).astype(bf16)
        p_hi, p_lo = split2(gf * y)
        gy_ref[at] += mm(p_hi, pick) + mm(p_lo, pick)
        eg_hi, eg_lo = split2(ea * gf)
        dc_ref[at] += mm_nt(eg_hi, st_hi) + (mm_nt(eg_hi, st_lo) + mm_nt(eg_lo, st_hi))
        wv_hi, wv_lo = split2(w * vf)
        btc = bt_ref[:, at]
        st = ea[LANES - 1 : LANES] * st + (mm(btc, wv_hi) + mm(btc, wv_lo))
    ut = ut_ref[...]
    final = jnp.sum(st * ut, axis=0, keepdims=True)
    e0, e1, e2 = split3(jnp.broadcast_to(final, (8, LANES)))
    end_ref[...] += (mm(e2, pick) + mm(e1, pick)) + mm(e0, pick)
    for c in reversed(range(chunks)):
        at = slice(c * LANES, (c + 1) * LANES)
        vf = v_ref[at].astype(f32)
        gf = g_ref[at].astype(f32)
        ea = ea_ref[at]
        w = w_ref[at]
        ut_hi, ut_lo = split2(ut)
        dv = dvi_ref[at] + w * (mm(b_ref[at], ut_hi) + mm(b_ref[at], ut_lo))
        gval_ref[at] = (dv + skip * gf).astype(bf16)
        p_hi, p_lo = split2(vf * dv)
        vdv_ref[at] += mm(p_hi, pick) + mm(p_lo, pick)
        wv_hi, wv_lo = split2(w * vf)
        db_ref[at] += mm_nt(wv_hi, ut_hi) + (mm_nt(wv_hi, ut_lo) + mm_nt(wv_lo, ut_hi))
        eg_hi, eg_lo = split2(ea * gf)
        ctc = ct_ref[:, at]
        ut = ea[LANES - 1 : LANES] * ut + (mm(ctc, eg_hi) + mm(ctc, eg_lo))


def finish_kernel(count, *refs):
    parts = [refs[6 * i : 6 * i + 6] for i in range(count)]
    b_ref, c_ref, dt_ref, sig_ref, dlog_ref, glog_ref, keys_ref = refs[6 * count :]
    rows = b_ref.shape[0]
    n = b_ref.shape[1]
    heads = glog_ref.shape[1]

    def total(i, at):
        out = parts[0][i][at]
        for part in parts[1:]:
            out = out + part[i][at]
        return out

    rate = -jnp.exp(dlog_ref[...])
    tri = jnp.where(iota((LANES, LANES), 0) <= iota((LANES, LANES), 1), 1.0, 0.0).astype(bf16)
    off = total(5, slice(0, 1))
    for c in reversed(range(rows // LANES)):
        at = slice(c * LANES, (c + 1) * LANES)
        vdv = total(4, at)
        q0, q1, q2 = split3(total(3, at) - vdv)
        run = (mm(tri, q2) + mm(tri, q1)) + mm(tri, q0) + off
        off = run[0:1]
        glog = (vdv / dt_ref[at] + rate * run) * sig_ref[at]
        glog_ref[at] = glog[:, :heads]
        z = total(0, at)
        z_hi, z_lo = split2(z)
        t_hi, t_lo = split2(z.T)
        keys_ref[at, n:] = total(1, at) + (mm(z_hi, b_ref[at]) + mm(z_lo, b_ref[at]))
        keys_ref[at, :n] = total(2, at) + (mm(t_hi, c_ref[at]) + mm(t_lo, c_ref[at]))


def exchange(payload, init, lo_count, hi_count, reverse):
    size = lo_count * hi_count
    q = payload.shape[1] - 8
    groups = [[z * lo_count + k for k in range(lo_count)] for z in range(hi_count)]
    parts = lax.all_to_all(
        payload, "seq", split_axis=0, concat_axis=0, tiled=True, axis_index_groups=groups
    )
    order = list(range(lo_count))
    if reverse:
        order = order[::-1]
    state = parts[order[0], :q]
    keep = parts[order[0], q : q + 8]
    for k in order[1:]:
        state = parts[k, q : q + 1] * state + parts[k, :q]
        keep = parts[k, q : q + 8] * keep
    mine = jnp.concatenate([state, keep], axis=0)
    z = lax.axis_index("seq") // lo_count
    got = []
    for e in range(1, hi_count):
        step = -e * lo_count if reverse else e * lo_count
        perm = [(i, i + step) for i in range(size) if 0 <= i + step < size]
        got.append(lax.ppermute(mine, "seq", perm))
    acc = init
    for e in range(hi_count - 1, 0, -1):
        there = (z + e < hi_count) if reverse else (z - e >= 0)
        other = got[e - 1]
        acc = jnp.where(there, other[q : q + 1] * acc + other[:q], acc)
    starts = [None] * lo_count
    for k in order:
        starts[k] = acc
        acc = parts[k, q : q + 1] * acc + parts[k, :q]
    out = lax.all_to_all(
        jnp.stack(starts), "seq", split_axis=0, concat_axis=0, tiled=True, axis_index_groups=groups
    )
    return out.reshape(lo_count * q, out.shape[2])


def body(
    token_values, step_logits, write_keys, read_queries, target, doc_lengths,
    decay_log, step_bias, skip_gain, init_state, out_grad,
):
    rows = token_values.shape[0]
    size = lax.axis_size("seq")
    me = lax.axis_index("seq")
    heads = decay_log.shape[0]
    width = token_values.shape[1]
    head_width = width // heads
    n = write_keys.shape[1]
    capacity = 2 * rows // size
    slots = size * capacity
    pairs = width // LANES
    assert head_width * 2 == LANES and n == LANES and heads <= LANES - 3
    assert rows & (rows - 1) == 0 and rows % LANES == 0
    lo_count = 4 if size % 4 == 0 else 1
    hi_count = size // lo_count
    q = n // lo_count

    local = target % rows
    marks = jnp.stack([local // 16, local % 16, jnp.ones_like(local)], axis=1).astype(bf16)
    kaux = jnp.concatenate(
        [
            write_keys,
            read_queries,
            step_logits,
            jnp.zeros((rows, LANES - 3 - heads), bf16),
            marks,
        ],
        axis=1,
    )
    kw = kaux.shape[1]
    onehot, kslots = pl.pallas_call(
        partial(dispatch_kernel, rows.bit_length() - 1, capacity),
        out_shape=(
            jax.ShapeDtypeStruct((slots, rows), bf16),
            jax.ShapeDtypeStruct((slots, kw), bf16),
        ),
        compiler_params=pltpu.CompilerParams(vmem_limit_bytes=56 * 1024 * 1024),
        name="dispatch",
    )(target.reshape(1, rows), target.reshape(rows, 1), kaux)

    def route(x):
        wide = x.reshape(size, capacity, x.shape[1])
        wide = lax.all_to_all(wide, "seq", split_axis=0, concat_axis=0, tiled=True)
        return wide.reshape(slots, x.shape[1])

    got_keys = route(kslots)
    count = min(GROUPS, pairs)
    edges = [pairs * i // count for i in range(count + 1)]
    spans = list(zip(edges[:-1], edges[1:]))
    got_values = []
    for lower, upper in spans:
        part = token_values[:, lower * LANES : upper * LANES]
        got_values.append(route(jnp.dot(onehot, part, preferred_element_type=f32).astype(bf16)))

    pad = (0, LANES - heads)
    bias_row = jnp.pad(step_bias, pad).reshape(1, LANES)
    dlog_row = jnp.pad(decay_log, pad).reshape(1, LANES)
    skip_row = jnp.broadcast_to(jnp.repeat(skip_gain, head_width)[None, :], (8, width))
    idx = jnp.reshape(me, (1,)).astype(jnp.int32)
    smem = pl.BlockSpec(memory_space=pltpu.SMEM)
    col = pl.BlockSpec((rows, LANES), lambda j: (0, j))
    tiles = whole((rows // LANES, LANES, LANES))

    def sds(shape, dtype=f32):
        return jax.ShapeDtypeStruct(shape, dtype)

    (pm, b, c, bt, ct, dt, sig, at, btt, eat, wt, wdt, mb, keep, u_span) = pl.pallas_call(
        partial(setup_kernel, heads, lo_count),
        grid=(pairs,),
        in_specs=[smem, smem, whole((slots, kw)), col, whole((1, LANES)), whole((1, LANES))],
        out_specs=[
            whole((rows, slots)),
            whole((rows, n)), whole((rows, n)), whole((n, rows)), whole((n, rows)),
            whole((rows, LANES)), whole((rows, LANES)),
            tiles, tiles, tiles, tiles, tiles,
            whole((rows, LANES)),
            pl.BlockSpec((8, LANES), lambda j: (0, j)),
            pl.BlockSpec((lo_count, q + 8, LANES), lambda j: (0, 0, j)),
        ],
        out_shape=[
            sds((rows, slots), bf16),
            sds((rows, n), bf16), sds((rows, n), bf16), sds((n, rows), bf16), sds((n, rows), bf16),
            sds((rows, LANES)), sds((rows, LANES)),
            *[sds((rows // LANES, LANES, LANES))] * 5,
            sds((rows, LANES)),
            sds((8, width)),
            sds((lo_count, q + 8, width)),
        ],
        scratch_shapes=[pltpu.VMEM((rows // LANES, LANES, LANES), f32)],
        compiler_params=params(),
        name="setup",
    )(idx, doc_lengths, got_keys, out_grad, bias_row, dlog_row)

    lo_at = me % lo_count
    init_part = lax.dynamic_slice_in_dim(init_state, lo_at * q, q, axis=2)
    init_part = init_part.reshape(width, q).T
    zero_part = jnp.zeros_like(init_part)
    ut = exchange(u_span, zero_part, lo_count, hi_count, True)

    partials = []
    outs = []
    grads = []
    for (lower, upper), got in zip(spans, got_values):
        cols = (upper - lower) * LANES
        shifted = pl.BlockSpec((rows, LANES), lambda j, lower=lower: (0, lower + j))
        v, f_span = pl.pallas_call(
            partial(place_kernel, lower, lo_count),
            grid=(upper - lower,),
            in_specs=[
                pl.BlockSpec((slots, LANES), lambda j: (0, j)),
                whole((rows, slots)),
                tiles,
                whole((n, rows)),
                pl.BlockSpec((8, LANES), lambda j, lower=lower: (0, lower + j)),
            ],
            out_specs=[col, pl.BlockSpec((lo_count, q + 8, LANES), lambda j: (0, 0, j))],
            out_shape=[sds((rows, cols), bf16), sds((lo_count, q + 8, cols))],
            compiler_params=params(),
            name="place",
        )(got, pm, wdt, bt, keep)
        st = exchange(
            f_span, init_part[:, lower * LANES : upper * LANES], lo_count, hi_count, False
        )
        acc = whole((rows, LANES))
        res = pl.pallas_call(
            partial(layer_kernel, lower),
            grid=(upper - lower,),
            in_specs=[
                col,
                shifted,
                pl.BlockSpec((n, LANES), lambda j: (0, j)),
                pl.BlockSpec((n, LANES), lambda j, lower=lower: (0, lower + j)),
                tiles, tiles, tiles, tiles,
                whole((rows, n)), whole((rows, n)), whole((n, rows)), whole((n, rows)),
                whole((rows, LANES)),
                pl.BlockSpec((8, LANES), lambda j, lower=lower: (0, lower + j)),
            ],
            out_specs=[col, col, acc, acc, acc, acc, acc, whole((8, LANES))],
            out_shape=[
                sds((rows, cols), bf16), sds((rows, cols), bf16),
                sds((rows, LANES)), sds((rows, LANES)), sds((rows, LANES)),
                sds((rows, LANES)), sds((rows, LANES)), sds((8, LANES)),
            ],
            scratch_shapes=[pltpu.VMEM((rows, LANES), f32)] * 4,
            compiler_params=params(),
            name="layer",
        )(v, out_grad, st, ut, at, btt, eat, wt, b, c, bt, ct, mb, skip_row)
        outs.append(res[0])
        grads.append(res[1])
        partials.extend(res[2:])

    grad_logits, keys_grad = pl.pallas_call(
        partial(finish_kernel, count),
        out_shape=[sds((rows, heads)), sds((rows, 2 * n))],
        compiler_params=pltpu.CompilerParams(vmem_limit_bytes=56 * 1024 * 1024),
        name="finish",
    )(*partials, b, c, dt, sig, dlog_row)
    if lax.axis_size("head") == 2:
        keys_grad = keys_grad + lax.ppermute(keys_grad, "head", [(0, 1), (1, 0)])
    else:
        keys_grad = lax.psum(keys_grad, "head")
    layer_out = outs[0] if count == 1 else jnp.concatenate(outs, axis=1)
    grad_values = grads[0] if count == 1 else jnp.concatenate(grads, axis=1)
    return layer_out, grad_values, grad_logits, keys_grad[:, :n], keys_grad[:, n:]


def solution(mesh):
    return jax.shard_map(
        body,
        mesh=mesh,
        in_specs=(
            P("seq", "head"),
            P("seq", "head"),
            P("seq", None),
            P("seq", None),
            P("seq"),
            P(),
            P("head"),
            P("head"),
            P("head"),
            P("head", None, None),
            P("seq", "head"),
        ),
        out_specs=(
            P("seq", "head"),
            P("seq", "head"),
            P("seq", "head"),
            P("seq", None),
            P("seq", None),
        ),
        check_vma=False,
    )
```

```python
from functools import partial

import jax
import jax.numpy as jnp
from jax import lax
from jax.experimental import pallas as pl
from jax.experimental.pallas import tpu as pltpu
from jax.sharding import PartitionSpec as P


f32 = jnp.float32
bf16 = jnp.bfloat16
LANES = 128
NEG = -1e30
LOG2E = 1.4426950408889634
LO = 4
SHARES = (4, 4, 4)
TAIL = 1


def split2(x):
    hi = x.astype(bf16)
    return hi, (x - hi.astype(f32)).astype(bf16)


def split3(x):
    hi = x.astype(bf16)
    rest = x - hi.astype(f32)
    mid = rest.astype(bf16)
    return hi, mid, (rest - mid.astype(f32)).astype(bf16)


def mm(a, b):
    return lax.dot_general(a, b, (((1,), (0,)), ((), ())), preferred_element_type=f32)


def mm_nt(a, b):
    return lax.dot_general(a, b, (((1,), (1,)), ((), ())), preferred_element_type=f32)


def iota(shape, dim):
    return lax.broadcasted_iota(jnp.int32, shape, dim)


def params(grid_dims=1):
    return pltpu.CompilerParams(
        dimension_semantics=("arbitrary",) * grid_dims, vmem_limit_bytes=56 * 1024 * 1024
    )


def whole(shape):
    return pl.BlockSpec(shape, lambda *_: (0,) * len(shape))


def dispatch_kernel(
    shift, capacity, split, idx_ref, trow_ref, write_ref, read_ref, logits_ref, oh_ref, ks_ref
):
    rows = trow_ref.shape[1]
    slots = oh_ref.shape[0]
    n = write_ref.shape[1]
    heads = logits_ref.shape[1]
    trow = trow_ref[...]
    owner_row = lax.shift_right_logical(trow, shift)
    local = (trow - lax.shift_left(owner_row, shift)).astype(f32)
    owner_f = jnp.broadcast_to(owner_row.astype(f32), (rows, rows))
    earlier = (owner_f.T == owner_f) & (iota((rows, rows), 0) < iota((rows, rows), 1))
    rank = jnp.sum(jnp.where(earlier, 1.0, 0.0), axis=0, keepdims=True)
    slot = owner_row * capacity + rank.astype(jnp.int32)
    onehot = jnp.where(iota((slots, rows), 0) == slot, 1.0, 0.0).astype(bf16)
    oh_ref[...] = onehot
    high = jnp.floor(local * (1.0 / 16.0))
    sub = iota((LANES, rows), 0)
    marks = jnp.where(
        sub == LANES - 3, high, jnp.where(sub == LANES - 2, local - 16.0 * high, 1.0)
    ).T
    wide = jnp.where(iota((heads, LANES), 0) == iota((heads, LANES), 1), 1.0, 0.0).astype(bf16)
    lane = iota((rows, LANES), 1)
    aux = jnp.where(lane >= LANES - 3, marks, mm(logits_ref[...], wide)).astype(bf16)
    ks_ref[:, :LANES] = mm(onehot, aux).astype(bf16)
    if split:
        key = jnp.where(idx_ref[3] == 0, write_ref[...], read_ref[...])
        ks_ref[:, LANES:] = mm(onehot, key).astype(bf16)
    else:
        ks_ref[:, LANES : LANES + n] = mm(onehot, write_ref[...]).astype(bf16)
        ks_ref[:, LANES + n :] = mm(onehot, read_ref[...]).astype(bf16)


def doc_at(docs_ref, pos):
    start = jnp.int32(0)
    total = pos * 0
    for d in range(docs_ref.shape[0] - 1):
        start = start + docs_ref[d]
        total = total + jnp.where(pos >= start, 1, 0)
    return total


def row_of(ref, c, h):
    return jnp.broadcast_to(ref[c, pl.ds(h, 1), :], (LANES, LANES))


def expand_pair(ref, c, h0):
    upper = iota((LANES, LANES), 0) < LANES // 2
    return jnp.where(upper, row_of(ref, c, h0), row_of(ref, c, h0 + 1)).T


def expand_all(ref, h0):
    return jnp.concatenate([expand_pair(ref, c, h0) for c in range(ref.shape[0])], axis=0)


def setup_kernel(
    heads, split, idx_ref, docs_ref, got_ref, other_ref, heads_ref,
    pm_ref, b_ref, c_ref, bt_ref, ct_ref, dt_ref, sig_ref, at_ref, btt_ref, eat_ref, wt_ref,
    wdt_ref, eadt_ref, mb_ref, skip_ref,
):
    rows = b_ref.shape[0]
    slots = got_ref.shape[0]
    n = b_ref.shape[1]
    chunks = rows // LANES
    p0 = idx_ref[0] * rows
    aux = got_ref[:, :LANES]
    aux_t = aux.astype(f32).T
    pos = aux_t[LANES - 3 : LANES - 2] * 16.0 + aux_t[LANES - 2 : LANES - 1]
    pos = jnp.where(aux_t[LANES - 1 : LANES] > 0.5, pos, -1.0).astype(jnp.int32)
    pm = jnp.where(iota((rows, slots), 0) == pos, 1.0, 0.0).astype(bf16)
    pm_ref[...] = pm
    if split:
        mine = mm(pm, got_ref[:, LANES:])
        other = mm(pm, other_ref[...])
        first = idx_ref[3] == 0
        b_all = jnp.where(first, mine, other)
        c_all = jnp.where(first, other, mine)
    else:
        b_all = mm(pm, got_ref[:, LANES : LANES + n])
        c_all = mm(pm, got_ref[:, LANES + n :])
    b_ref[...] = b_all.astype(bf16)
    c_ref[...] = c_all.astype(bf16)
    logits = jnp.where(iota((rows, LANES), 1) < heads, mm(pm, aux), 0.0)
    x = logits + heads_ref[0:1]
    u = jnp.exp(-jnp.abs(x))
    small = u * (1.0 - u * (0.5 - u * (1.0 / 3.0 - u * (0.25 - u * 0.2))))
    dt = jnp.maximum(x, 0.0) + jnp.where(u < 0.03, small, jnp.log(1.0 + u))
    dt_ref[...] = dt
    sig_ref[...] = jnp.where(x >= 0.0, 1.0, u) / (1.0 + u)
    logdt = jnp.log(dt) * LOG2E
    z = dt * (-jnp.exp(heads_ref[1:2]) * LOG2E)
    tri = jnp.where(iota((LANES, LANES), 0) >= iota((LANES, LANES), 1), 1.0, 0.0).astype(bf16)
    offs = []
    off = jnp.zeros((1, LANES), f32)
    local = []
    for c in range(chunks):
        z0, z1, z2 = split3(z[c * LANES : (c + 1) * LANES])
        a = (mm(tri, z2) + mm(tri, z1)) + mm(tri, z0)
        local.append(a)
        offs.append(off)
        off = off + a[LANES - 1 : LANES]
    doc_before = doc_at(docs_ref, p0 - 1)
    doc_last = doc_at(docs_ref, p0 + rows - 1)
    for c in range(chunks):
        at = slice(c * LANES, (c + 1) * LANES)
        q0 = p0 + c * LANES
        a = local[c]
        ld = logdt[at]
        end = a[LANES - 1 : LANES]
        doc_n = doc_at(docs_ref, q0 + iota((LANES, LANES), 0))
        doc_t = doc_at(docs_ref, q0 + iota((LANES, LANES), 1))
        causal = (doc_n == doc_t) & (iota((LANES, LANES), 0) >= iota((LANES, LANES), 1))
        mb_ref[at] = jnp.where(causal, 0.0, NEG)
        at_ref[c] = a.T
        btt_ref[c] = (a - ld).T
        eat_ref[c] = jnp.where(doc_n == doc_at(docs_ref, q0 - 1), a, NEG).T
        wt_ref[c] = jnp.where(
            doc_n == doc_at(docs_ref, q0 + LANES - 1), end - a + ld, NEG
        ).T
        full = a + offs[c]
        eadt_ref[c] = jnp.where(doc_n == doc_before, full, NEG).T
        wdt_ref[c] = jnp.where(doc_n == doc_last, off - full + ld, NEG).T
        bt_ref[:, at] = b_all[at].T.astype(bf16)
        ct_ref[:, at] = c_all[at].T.astype(bf16)
    width = skip_ref.shape[1]
    to_lanes = jnp.where(
        iota((LANES, width), 0) == lax.shift_right_logical(iota((LANES, width), 1), 6), 1.0, 0.0
    ).astype(bf16)
    s0, s1, s2 = split3(jnp.broadcast_to(heads_ref[2:3], (8, LANES)))
    skip_ref[...] = (mm(s2, to_lanes) + mm(s1, to_lanes)) + mm(s0, to_lanes)


def place_kernel(base, fresh, idx_ref, got_ref, g_ref, pm_ref, wdt_ref, eadt_ref, bt_ref, ct_ref, *refs):
    if not fresh:
        refs = refs[LO:]
    v_ref, outs, (f_ref, u_ref) = refs[0], refs[1 : 1 + LO], refs[1 + LO :]
    rows = v_ref.shape[0]
    v = mm(pm_ref[...], got_ref[...])
    v_ref[...] = v.astype(bf16)
    wide = v.shape[1] // LANES
    h0 = 2 * (base + wide * pl.program_id(0))
    w = jnp.concatenate([expand_all(wdt_ref, h0 + 2 * i) for i in range(wide)], axis=1)
    hi, lo = split2(jnp.exp2(w) * v)
    f_ref[...] = mm(bt_ref[...], hi) + mm(bt_ref[...], lo)
    ea = jnp.concatenate([expand_all(eadt_ref, h0 + 2 * i) for i in range(wide)], axis=1)
    ea = jnp.exp2(ea)
    hi, lo = split2(ea * g_ref[...].astype(f32))
    u_ref[...] = mm(ct_ref[...], hi) + mm(ct_ref[...], lo)
    keep = jnp.broadcast_to(ea[rows - 1 : rows], (8, ea.shape[1]))
    q = f_ref.shape[0] // LO
    for d, ref in enumerate(outs):
        at = pl.multiple_of(lax.bitwise_xor(idx_ref[1], d) * q, q)
        ref[0, :q, :] = f_ref[pl.ds(at, q), :]
        ref[1, :q, :] = u_ref[pl.ds(at, q), :]
        ref[0, q:, :] = keep
        ref[1, q:, :] = keep


def sort_parts(mine, part_refs, sorted_ref):
    for d, ref in enumerate(part_refs):
        sorted_ref[lax.bitwise_xor(mine, d)] = ref[...]


def total_kernel(idx_ref, p0_ref, p1_ref, p2_ref, p3_ref, *refs):
    outs, sorted_ref = refs[:-1], refs[-1]
    q = sorted_ref.shape[2] - 8
    sort_parts(idx_ref[1], (p0_ref, p1_ref, p2_ref, p3_ref), sorted_ref)
    totals = []
    for way in range(2):
        order = list(range(LO))[::-1] if way else list(range(LO))
        state = sorted_ref[order[0], way, :q]
        keep = sorted_ref[order[0], way, q:]
        for k in order[1:]:
            state = sorted_ref[k, way, q : q + 1] * state + sorted_ref[k, way, :q]
            keep = sorted_ref[k, way, q:] * keep
        totals.append((state, keep))
    z = idx_ref[2]
    for e, ref in enumerate(outs, 1):
        up = lax.bitwise_xor(z, e) > z
        ref[:q] = jnp.where(up, totals[0][0], totals[1][0])
        ref[q:] = jnp.where(up, totals[0][1], totals[1][1])


def starts_kernel(lower, others, idx_ref, p0_ref, p1_ref, p2_ref, p3_ref, init_ref, *refs):
    got = refs[:others]
    outs = refs[others : others + LO]
    sorted_ref, far_ref, made_ref = refs[others + LO :]
    q = made_ref.shape[2]
    cols = made_ref.shape[3]
    z = idx_ref[2]
    sort_parts(idx_ref[1], (p0_ref, p1_ref, p2_ref, p3_ref), sorted_ref)
    for e, ref in enumerate(got, 1):
        far_ref[lax.bitwise_xor(z, e)] = ref[...]
    for way in range(2):
        if way:
            acc = jnp.zeros((q, cols), f32)
        else:
            acc = init_ref[:, lower * LANES : lower * LANES + cols]
        planes = list(range(others + 1))
        order = list(range(LO))
        if way:
            planes, order = planes[::-1], order[::-1]
        for p in planes:
            there = (p > z) if way else (p < z)
            acc = jnp.where(there, far_ref[p, q : q + 1] * acc + far_ref[p, :q], acc)
        for k in order:
            made_ref[k, way] = acc
            acc = sorted_ref[k, way, q : q + 1] * acc + sorted_ref[k, way, :q]
    for d, ref in enumerate(outs):
        ref[...] = made_ref[lax.bitwise_xor(idx_ref[1], d)]


def join_quarters(idx_ref, part_refs, way, whole_ref):
    q = part_refs[0].shape[1]
    for d, ref in enumerate(part_refs):
        at = pl.multiple_of(lax.bitwise_xor(idx_ref[1], d) * q, q)
        whole_ref[pl.ds(at, q), :] = ref[way]


def inner_kernel(
    base, v_ref, g_ref, at_ref, btt_ref, b_ref, c_ref, mb_ref,
    yi_ref, dvi_ref, z_ref, cb_ref,
):
    chunks = v_ref.shape[0] // LANES
    half = LANES // 2
    j = pl.program_id(0)
    h0 = 2 * (base + j)

    @pl.when(j == 0)
    def _():
        for c in range(chunks):
            at = slice(c * LANES, (c + 1) * LANES)
            cb_ref[at] = mm_nt(c_ref[at], b_ref[at])
        z_ref[...] = jnp.zeros_like(z_ref)

    low = iota((LANES, LANES), 1) < half
    for c in range(chunks):
        at = slice(c * LANES, (c + 1) * LANES)
        v = v_ref[at]
        g = g_ref[at]
        zero = jnp.zeros_like(v)
        gt = g.astype(f32).T.astype(bf16)
        cb = cb_ref[at]
        mb = mb_ref[at]
        zacc = z_ref[at]
        his, los, dvs = [], [], []
        for k in range(2):
            acol = row_of(at_ref, c, h0 + k).T
            spread = jnp.exp2(acol - row_of(btt_ref, c, h0 + k) + mb)
            mine = low if k == 0 else jnp.logical_not(low)
            gv = mm_nt(jnp.where(mine, g, zero), v)
            zacc = zacc + gv * spread
            hi, lo = split2(cb * spread)
            his.append(hi)
            los.append(lo)
            gk = gt[k * half : (k + 1) * half]
            dvs.append(mm(gk, hi) + mm(gk, lo))
        z_ref[at] = zacc
        dvi_ref[at] = jnp.concatenate(dvs, axis=0).T
        both = jnp.concatenate([jnp.where(low, v, zero), jnp.where(low, zero, v)], axis=0)
        yi_ref[at] = mm(jnp.concatenate(his, axis=1), both) + mm(
            jnp.concatenate(los, axis=1), both
        )


def outer_kernel(
    base, fresh, idx_ref, v_ref, g_ref, yi_ref, dvi_ref, s0_ref, s1_ref, s2_ref, s3_ref,
    eat_ref, wt_ref, b_ref, c_ref, bt_ref, ct_ref, skip_ref, *refs,
):
    if not fresh:
        refs = refs[2:]
    lout_ref, gval_ref, dc_ref, db_ref, gy_ref, vdv_ref, end_ref = refs[:7]
    ea_ref, w_ref, st_ref, ut_ref = refs[7:]
    chunks = v_ref.shape[0] // LANES
    block = v_ref.shape[1]
    wide = block // LANES
    j = pl.program_id(0)
    h0 = 2 * (base + wide * j)

    def factors(ref, c):
        return jnp.exp2(
            jnp.concatenate([expand_pair(ref, c, h0 + 2 * i) for i in range(wide)], axis=1)
        )

    @pl.when(j == 0)
    def _():
        for ref in (dc_ref, db_ref, gy_ref, vdv_ref, end_ref):
            ref[...] = jnp.zeros_like(ref)

    head_of = h0 + lax.shift_right_logical(iota((block, LANES), 0), 6)
    pick = jnp.where(head_of == iota((block, LANES), 1), 1.0, 0.0).astype(bf16)
    skip = skip_ref[0:1]
    join_quarters(idx_ref, (s0_ref, s1_ref, s2_ref, s3_ref), 0, st_ref)
    join_quarters(idx_ref, (s0_ref, s1_ref, s2_ref, s3_ref), 1, ut_ref)
    st = st_ref[...]
    for c in range(chunks):
        at = slice(c * LANES, (c + 1) * LANES)
        vf = v_ref[at].astype(f32)
        gf = g_ref[at].astype(f32)
        ea = factors(eat_ref, c)
        w = factors(wt_ref, c)
        ea_ref[at] = ea
        w_ref[at] = w
        st_hi, st_lo = split2(st)
        y = yi_ref[at] + ea * (mm(c_ref[at], st_hi) + mm(c_ref[at], st_lo))
        lout_ref[at] = (y + skip * vf).astype(bf16)
        p_hi, p_lo = split2(gf * y)
        gy_ref[at] += mm(p_hi, pick) + mm(p_lo, pick)
        eg_hi, eg_lo = split2(ea * gf)
        dc_ref[at] += mm_nt(eg_hi, st_hi) + (mm_nt(eg_hi, st_lo) + mm_nt(eg_lo, st_hi))
        wv_hi, wv_lo = split2(w * vf)
        btc = bt_ref[:, at]
        st = ea[LANES - 1 : LANES] * st + (mm(btc, wv_hi) + mm(btc, wv_lo))
    ut = ut_ref[...]
    final = jnp.sum(st * ut, axis=0, keepdims=True)
    e0, e1, e2 = split3(jnp.broadcast_to(final, (8, block)))
    end_ref[...] += (mm(e2, pick) + mm(e1, pick)) + mm(e0, pick)
    for c in reversed(range(chunks)):
        at = slice(c * LANES, (c + 1) * LANES)
        vf = v_ref[at].astype(f32)
        gf = g_ref[at].astype(f32)
        ea = ea_ref[at]
        w = w_ref[at]
        ut_hi, ut_lo = split2(ut)
        dv = dvi_ref[at] + w * (mm(b_ref[at], ut_hi) + mm(b_ref[at], ut_lo))
        gval_ref[at] = (dv + skip * gf).astype(bf16)
        p_hi, p_lo = split2(vf * dv)
        vdv_ref[at] += mm(p_hi, pick) + mm(p_lo, pick)
        wv_hi, wv_lo = split2(w * vf)
        db_ref[at] += mm_nt(wv_hi, ut_hi) + (mm_nt(wv_hi, ut_lo) + mm_nt(wv_lo, ut_hi))
        eg_hi, eg_lo = split2(ea * gf)
        ctc = ct_ref[:, at]
        ut = ea[LANES - 1 : LANES] * ut + (mm(ctc, eg_hi) + mm(ctc, eg_lo))


def finish_kernel(inner, outer, *refs):
    zs = refs[:inner]
    parts = [refs[inner + 5 * i : inner + 5 * i + 5] for i in range(outer)]
    b_ref, c_ref, dt_ref, sig_ref, heads_ref, glog_ref, keys_ref = refs[inner + 5 * outer :]
    rows = b_ref.shape[0]
    n = b_ref.shape[1]
    heads = glog_ref.shape[1]

    def total(i, at):
        out = parts[0][i][at]
        for part in parts[1:]:
            out = out + part[i][at]
        return out

    rate = -jnp.exp(heads_ref[1:2])
    tri = jnp.where(iota((LANES, LANES), 0) <= iota((LANES, LANES), 1), 1.0, 0.0).astype(bf16)
    off = total(4, slice(0, 1))
    for c in reversed(range(rows // LANES)):
        at = slice(c * LANES, (c + 1) * LANES)
        vdv = total(3, at)
        q0, q1, q2 = split3(total(2, at) - vdv)
        run = (mm(tri, q2) + mm(tri, q1)) + mm(tri, q0) + off
        off = run[0:1]
        glog = (vdv / dt_ref[at] + rate * run) * sig_ref[at]
        glog_ref[at] = glog[:, :heads]
        z = zs[0][at]
        for ref in zs[1:]:
            z = z + ref[at]
        z_hi, z_lo = split2(z)
        t_hi, t_lo = split2(z.T)
        keys_ref[at, n:] = total(0, at) + (mm(z_hi, b_ref[at]) + mm(z_lo, b_ref[at]))
        keys_ref[at, :n] = total(1, at) + (mm(t_hi, c_ref[at]) + mm(t_lo, c_ref[at]))


def in_group(size, d):
    return [(i, i - i % LO + ((i % LO) ^ d)) for i in range(size)]


def body(
    token_values, step_logits, write_keys, read_queries, target, doc_lengths,
    decay_log, step_bias, skip_gain, init_state, out_grad,
):
    rows = token_values.shape[0]
    size = lax.axis_size("seq")
    me = lax.axis_index("seq")
    heads = decay_log.shape[0]
    width = token_values.shape[1]
    head_width = width // heads
    n = write_keys.shape[1]
    capacity = 2 * rows // size
    slots = size * capacity
    pairs = width // LANES
    assert head_width * 2 == LANES and n == LANES and heads <= LANES - 3
    assert rows & (rows - 1) == 0 and rows % LANES == 0 and size % LO == 0
    hi_count = size // LO
    others = hi_count - 1
    q = n // LO
    chunks = rows // LANES
    vmem = pltpu.CompilerParams(vmem_limit_bytes=56 * 1024 * 1024)

    def sds(shape, dtype=f32):
        return jax.ShapeDtypeStruct(shape, dtype)

    split = lax.axis_size("head") == 2
    kw = LANES + (n if split else 2 * n)
    idx = jnp.stack([me, me % LO, me // LO, lax.axis_index("head")]).astype(jnp.int32)
    smem = pl.BlockSpec(memory_space=pltpu.SMEM)
    anywhere = pl.BlockSpec(memory_space=pl.ANY)
    full = pl.BlockSpec(memory_space=pltpu.VMEM)
    tiles = whole((chunks, LANES, LANES))
    tile_shape = sds((chunks, LANES, LANES))

    onehot, kslots = pl.pallas_call(
        partial(dispatch_kernel, rows.bit_length() - 1, capacity, split),
        in_specs=[smem, full, full, full, full],
        out_shape=(sds((slots, rows), bf16), sds((slots, kw), bf16)),
        compiler_params=vmem,
        name="dispatch",
    )(idx, target.reshape(1, rows), write_keys, read_queries, step_logits)

    def route(x):
        there = x.reshape(size, capacity, x.shape[1])
        there = lax.all_to_all(there, "seq", split_axis=0, concat_axis=0, tiled=True)
        return there.reshape(slots, x.shape[1])

    got_keys = route(kslots)
    spans = make_plan(pairs)
    sent = []
    for lower, upper in spans:
        part = token_values[:, lower * LANES : upper * LANES]
        sent.append(jnp.dot(onehot, part, preferred_element_type=f32).astype(bf16))
    got_values = [route(part) for part in sent]

    per_head = jnp.pad(
        jnp.stack([step_bias, decay_log, skip_gain]), ((0, 5), (0, LANES - heads))
    )
    if split:
        other = lax.ppermute(got_keys[:, LANES:], "head", [(0, 1), (1, 0)])
    else:
        other = got_keys
    (
        pm, b, c, bt, ct, dt, sig, at, btt, eat, wt, wdt, eadt, mb, skip_row
    ) = pl.pallas_call(
        partial(setup_kernel, heads, split),
        in_specs=[smem, smem, full, full, full],
        out_shape=[
            sds((rows, slots), bf16),
            sds((rows, n), bf16), sds((rows, n), bf16),
            sds((n, rows), bf16), sds((n, rows), bf16),
            sds((rows, LANES)), sds((rows, LANES)),
            *[tile_shape] * 6,
            sds((rows, LANES)),
            sds((8, width)),
        ],
        compiler_params=vmem,
        name="setup",
    )(idx, doc_lengths, got_keys, other, per_head)

    init_part = lax.dynamic_slice_in_dim(init_state, (me % LO) * q, q, axis=2)
    init_part = init_part.reshape(width, q).T

    def ring(parts):
        out = [parts[0]]
        for d in range(1, LO):
            out.append(lax.ppermute(parts[d], "seq", in_group(size, d)))
        return out

    def exchange(parts, lower):
        cols = parts[0].shape[2]
        got = ring(parts)
        mine = pl.pallas_call(
            total_kernel,
            in_specs=[smem, *[full] * LO],
            out_shape=[sds((q + 8, cols))] * others,
            scratch_shapes=[pltpu.VMEM((LO, 2, q + 8, cols), f32)],
            compiler_params=vmem,
        )(idx, *got)
        far = []
        for e in range(1, hi_count):
            perm = [(i, ((i // LO) ^ e) * LO + i % LO) for i in range(size)]
            far.append(lax.ppermute(mine[e - 1], "seq", perm))
        starts = pl.pallas_call(
            partial(starts_kernel, lower, others),
            in_specs=[smem, *[full] * (LO + 1 + others)],
            out_shape=[sds((2, q, cols))] * LO,
            scratch_shapes=[
                pltpu.VMEM((LO, 2, q + 8, cols), f32),
                pltpu.VMEM((hi_count, q + 8, cols), f32),
                pltpu.VMEM((LO, 2, q, cols), f32),
            ],
            compiler_params=vmem,
        )(idx, *got, init_part, *far)
        return ring(starts)

    def blocking(lower, upper):
        many = 2 if (upper - lower) % 2 == 0 and lower % 2 == 0 else 1
        return many, many * LANES, (upper - lower) // many

    cut = max(len(spans) - TAIL, 0)
    teams = [t for t in (list(range(cut)), list(range(cut, len(spans)))) if t]
    placed = []
    zs = []
    inners = []
    payloads = {}
    for t, team in enumerate(teams):
        first, stop = spans[team[0]][0], spans[team[-1]][1]
        payload = None
        for i in team:
            lower, upper = spans[i]
            cols = (upper - lower) * LANES
            many, block, steps = blocking(lower, upper)
            inside = (lower - first) // many
            fresh = payload is None
            v, *payload = pl.pallas_call(
                partial(place_kernel, lower, fresh),
                grid=(steps,),
                in_specs=[
                    smem,
                    pl.BlockSpec((slots, block), lambda j: (0, j)),
                    pl.BlockSpec((rows, block), lambda j, o=lower // many: (0, o + j)),
                    whole((rows, slots)),
                    tiles, tiles, whole((n, rows)), whole((n, rows)),
                    *([] if fresh else [anywhere] * LO),
                ],
                out_specs=[
                    pl.BlockSpec((rows, block), lambda j: (0, j)),
                    *[pl.BlockSpec((2, q + 8, block), lambda j, o=inside: (0, 0, o + j))] * LO,
                ],
                out_shape=[
                    sds((rows, cols), bf16), *[sds((2, q + 8, (stop - first) * LANES))] * LO
                ],
                scratch_shapes=[pltpu.VMEM((n, block), f32)] * 2,
                input_output_aliases={} if fresh else {8 + d: 1 + d for d in range(LO)},
                compiler_params=params(),
            )(idx, got_values[i], out_grad, pm, wdt, eadt, bt, ct, *(payload or []))
            placed.append(v)
            col = pl.BlockSpec((rows, LANES), lambda j: (0, j))
            yi, dvi, z = pl.pallas_call(
                partial(inner_kernel, lower),
                grid=(upper - lower,),
                in_specs=[
                    col,
                    pl.BlockSpec((rows, LANES), lambda j, o=lower: (0, o + j)),
                    tiles, tiles, whole((rows, n)), whole((rows, n)), whole((rows, LANES)),
                ],
                out_specs=[col, col, whole((rows, LANES))],
                out_shape=[sds((rows, cols)), sds((rows, cols)), sds((rows, LANES))],
                scratch_shapes=[pltpu.VMEM((rows, LANES), f32)],
                compiler_params=params(),
            )(v, out_grad, at, btt, b, c, mb)
            inners.append((yi, dvi))
            zs.append(z)
        payloads[t] = (payload, first)

    states = {}
    for t, team in enumerate(teams):
        payload, first = payloads[t]
        st = exchange(payload, first)
        for i in team:
            states[i] = (st, first)

    partials = []
    made = None
    for i, (lower, upper) in enumerate(spans):
        cols = (upper - lower) * LANES
        many, block, steps = blocking(lower, upper)
        st, first = states[i]
        inside = (lower - first) // many
        acc = whole((rows, LANES))
        own = pl.BlockSpec((rows, block), lambda j: (0, j))
        shifted = pl.BlockSpec((rows, block), lambda j, o=lower // many: (0, o + j))
        res = pl.pallas_call(
            partial(outer_kernel, lower, made is None),
            grid=(steps,),
            in_specs=[
                smem, own, shifted, own, own,
                *[pl.BlockSpec((2, q, block), lambda j, o=inside: (0, 0, o + j))] * LO,
                tiles, tiles,
                whole((rows, n)), whole((rows, n)), whole((n, rows)), whole((n, rows)),
                pl.BlockSpec((8, block), lambda j, o=lower // many: (0, o + j)),
                *([] if made is None else [anywhere] * 2),
            ],
            out_specs=[shifted, shifted, acc, acc, acc, acc, whole((8, LANES))],
            out_shape=[
                sds((rows, width), bf16), sds((rows, width), bf16),
                *[sds((rows, LANES))] * 4, sds((8, LANES)),
            ],
            scratch_shapes=[
                pltpu.VMEM((rows, block), f32), pltpu.VMEM((rows, block), f32),
                pltpu.VMEM((n, block), f32), pltpu.VMEM((n, block), f32),
            ],
            input_output_aliases={} if made is None else {16: 0, 17: 1},
            compiler_params=params(),
        )(
            idx, placed[i], out_grad, *inners[i], *st, eat, wt, b, c, bt, ct, skip_row,
            *(made or ()),
        )
        made = (res[0], res[1])
        partials.extend(res[2:])

    grad_logits, keys_grad = pl.pallas_call(
        partial(finish_kernel, len(zs), len(spans)),
        out_shape=[sds((rows, heads)), sds((rows, 2 * n))],
        compiler_params=vmem,
        name="finish",
    )(*zs, *partials, b, c, dt, sig, per_head)
    if split:
        keys_grad = keys_grad + lax.ppermute(keys_grad, "head", [(0, 1), (1, 0)])
    else:
        keys_grad = lax.psum(keys_grad, "head")
    return made[0], made[1], grad_logits, keys_grad[:, :n], keys_grad[:, n:]


def make_plan(pairs):
    total = sum(SHARES)
    edges = [0]
    for share in SHARES:
        edges.append(edges[-1] + share)
    cuts = [pairs * e // total for e in edges]
    return [(a, b) for a, b in zip(cuts[:-1], cuts[1:]) if b > a]


def solution(mesh):
    return jax.shard_map(
        body,
        mesh=mesh,
        in_specs=(
            P("seq", "head"),
            P("seq", "head"),
            P("seq", None),
            P("seq", None),
            P("seq"),
            P(),
            P("head"),
            P("head"),
            P("head"),
            P("head", None, None),
            P("seq", "head"),
        ),
        out_specs=(
            P("seq", "head"),
            P("seq", "head"),
            P("seq", "head"),
            P("seq", None),
            P("seq", None),
        ),
        check_vma=False,
    )
```
